512 devices in a mesh: shard: 128 (over y, z, core), tensor: 4 (over x).
Axes of the slice: x: 4, y: 8, z: 8, core: 2. Of those that a mesh axis runs over, the one named last changes fastest.
Arguments:
- grads: float32 [256, 384, 384], P('tensor', 'shard'), may hold values from -0.3 to 0.3
- moment_one: float32 [512, 73728], P(('tensor', 'shard')), may hold values from -0.3 to 0.3
- moment_two: float32 [512, 73728], P(('tensor', 'shard')), may hold values from 0.0005 to 0.01
- left_stat: float32 [512, 73728], P(('tensor', 'shard')), may hold values from -1 to 9, as said below
- right_stat: float32 [512, 73728], P(('tensor', 'shard')), may hold values from -1 to 9, as said below
- left_basis: float32 [512, 73728], P(('tensor', 'shard')), may hold values from -1 to 2
- right_basis: float32 [512, 73728], P(('tensor', 'shard')), may hold values from -1 to 2
Outputs:
- update: float32 [256, 384, 384], P('tensor', 'shard')
- new_moment_one: float32 [512, 73728], P(('tensor', 'shard'))
- new_moment_two: float32 [512, 73728], P(('tensor', 'shard'))
- new_left_stat: float32 [512, 73728], P(('tensor', 'shard'))
- new_right_stat: float32 [512, 73728], P(('tensor', 'shard'))
- new_left_basis: float32 [512, 73728], P(('tensor', 'shard'))
- new_right_basis: float32 [512, 73728], P(('tensor', 'shard'))
The draws below stay inside these ranges and needn't reach their ends.
Inputs may be any that keep to these rules, and one draw needn't show every extreme that they name: `left_stat`: each tile of the statistics is symmetric. `right_stat`: each tile of the statistics is symmetric.
All inputs are finite; a program needn't handle non-finite values.
Results may differ from the reference program's by a relative error of at most 0.00024.
Values sent between devices are 32-bit elements; how exact they have to be, the bound alone decides.
A program may use at most 64 MiB of HBM per device.

```python
import math
import jax
import jax.numpy as jnp
from jax import lax

B = 384
HALF = 192
NS_ITERS = 5
TILES = 256
HALVES = 512


def to_halves_drawn(tiles):
    count = tiles.shape[0]
    return tiles.reshape(count, B, 2, HALF).transpose(0, 2, 1, 3).reshape(2 * count, B * HALF)


def identity_tiles():
    return (jnp.arange(B)[:, None] == jnp.arange(B)[None, :]).astype(jnp.float32)


def statistic(key):
    diag_key, noise_key = jax.random.split(key)
    diagonal = jnp.exp(jax.random.uniform(diag_key, (TILES, B), jnp.float32, math.log(0.5), math.log(5.0)))
    noise = jnp.clip(jax.random.normal(noise_key, (TILES, B, B), jnp.float32), -4.0, 4.0) * 0.05
    symmetric = noise + jnp.transpose(noise, (0, 2, 1))
    return to_halves_drawn(symmetric + identity_tiles()[None, :, :] * diagonal[:, :, None])


def basis(key):
    noise = jnp.clip(jax.random.normal(key, (TILES, B, B), jnp.float32), -4.0, 4.0) * (0.5 / math.sqrt(B))
    return to_halves_drawn(identity_tiles()[None, :, :] + noise)


def draw_left_stat(key, part):
    return statistic(jax.random.fold_in(key, 11))


def draw_right_stat(key, part):
    return statistic(jax.random.fold_in(key, 12))


def draw_left_basis(key, part):
    return basis(jax.random.fold_in(key, 13))


def draw_right_basis(key, part):
    return basis(jax.random.fold_in(key, 14))


def steps_of(stream_key, dims, cuts, low, largest):
    gain = 1.0
    for dim, blocks in cuts:
        heights = jax.random.uniform(jax.random.fold_in(jax.random.fold_in(stream_key, 6), dim), (blocks,), jnp.float32, low / len(cuts), largest / len(cuts))
        gain = gain * jnp.repeat(jnp.exp(heights), dims[dim] // blocks).reshape((-1,) + (1,) * (len(dims) - 1 - dim))
    return gain


def centred(stream_key, dims, scale, most, pieces=(), dtype=jnp.bfloat16):
    gain = steps_of(stream_key, dims, pieces, -0.22, 0.18) if pieces else 1.0
    entries = jax.random.normal(stream_key, dims, jnp.float32) * scale * gain
    return jnp.minimum(jnp.maximum(entries, -most), most).astype(dtype)


def setup_inputs(seed: int = 0) -> dict:
    keys = jax.random.split(jax.random.key(seed), 8)
    return {
        "grads": centred(keys[0], (TILES, B, B), 0.05, 0.3, ((0, 4), (1, 128)), jnp.float32),
        "moment_one": centred(keys[1], (HALVES, B * HALF), 0.05, 0.3, ((0, 512),), jnp.float32),
        "moment_two": jnp.clip(jnp.exp(math.log(0.01) - 2.9957322 * jax.random.uniform(keys[2], (HALVES, B * HALF), jnp.float32) ** steps_of(keys[2], (HALVES, B * HALF), ((0, 512),), -0.2, 0.2)), 0.0005, 0.01),
        "left_stat": draw_left_stat(jax.random.fold_in(keys[7], 71), 0),
        "right_stat": draw_right_stat(jax.random.fold_in(keys[7], 71), 0),
        "left_basis": draw_left_basis(jax.random.fold_in(keys[7], 71), 0),
        "right_basis": draw_right_basis(jax.random.fold_in(keys[7], 71), 0),
    }


HIGHEST_PRECISION = lax.Precision.HIGHEST
BETA_ONE = 0.9
BETA_TWO = 0.95
ADAM_EPS = 1e-08
NORM_EPS = 1e-06
LINEAR_COEFF = 3.4445
CUBIC_COEFF = -4.775
QUINTIC_COEFF = 2.0315

def matmul(first_matrix, second_matrix):
    return jnp.dot(first_matrix, second_matrix, precision=HIGHEST_PRECISION, preferred_element_type=jnp.float32)

def to_tiles(halves):
    count = halves.shape[0]
    return halves.reshape(count // 2, 2, B, HALF).transpose(0, 2, 1, 3).reshape(count // 2, B, 2 * HALF)

def to_halves(tiles):
    count = tiles.shape[0]
    return tiles.reshape(count, B, 2, HALF).transpose(0, 2, 1, 3).reshape(2 * count, B * HALF)

def orthogonalize(power):
    frobenius = jnp.sqrt(jnp.sum(power * power) + NORM_EPS)
    iterate = power / frobenius
    for iteration in range(NS_ITERS):
        gram = matmul(iterate, iterate.T)
        poly = CUBIC_COEFF * gram + QUINTIC_COEFF * matmul(gram, gram)
        iterate = LINEAR_COEFF * iterate + matmul(poly, iterate)
    return iterate

def one_tile(inputs):
    gradient, moment_first, moment_second, stat_left, stat_right, basis_left, basis_right = inputs
    rotated = matmul(matmul(basis_left.T, gradient), basis_right)
    new_first = BETA_ONE * moment_first + (1.0 - BETA_ONE) * rotated
    new_second = BETA_TWO * moment_second + (1.0 - BETA_TWO) * rotated * rotated
    direction = new_first / (jnp.sqrt(new_second) + ADAM_EPS)
    update = matmul(basis_left, matmul(direction, basis_right.T))
    new_left = 0.5 * stat_left + 0.5 * matmul(gradient, gradient.T)
    new_right = 0.5 * stat_right + 0.5 * matmul(gradient.T, gradient)
    refreshed_left = orthogonalize(matmul(new_left, basis_left))
    refreshed_right = orthogonalize(matmul(new_right, basis_right))
    return (update, new_first, new_second, new_left, new_right, refreshed_left, refreshed_right)

def reference(grads, moment_one, moment_two, left_stat, right_stat, left_basis, right_basis):
    inputs = (grads, to_tiles(moment_one), to_tiles(moment_two), to_tiles(left_stat), to_tiles(right_stat), to_tiles(left_basis), to_tiles(right_basis))
    results = lax.map(one_tile, inputs)
    return (results[0], to_halves(results[1]), to_halves(results[2]), to_halves(results[3]), to_halves(results[4]), to_halves(results[5]), to_halves(results[6]))
```

```python
import jax
import jax.numpy as jnp
from jax import lax
from jax.experimental import pallas as pl
from jax.experimental.pallas import tpu as pltpu
from jax.sharding import PartitionSpec as P

NS_ITERS = 5
BETA_ONE = 0.9
BETA_TWO = 0.95
ADAM_EPS = 1e-08
NORM_EPS = 1e-06
LINEAR_COEFF = 3.4445
CUBIC_COEFF = -4.775
QUINTIC_COEFF = 2.0315

B = 384
LINES = 576
MESH = pl.DeviceIdType.MESH
F32 = jnp.float32
BF16 = jnp.bfloat16
NN = (((1,), (0,)), ((), ()))
NT = (((1,), (1,)), ((), ()))


def split(x):
    high = x.astype(BF16)
    return high, (x - high.astype(F32)).astype(BF16)


def dot(a, b, dims=NN):
    left = jnp.concatenate([a[0], a[0], a[1]], dims[0][0][0])
    right = jnp.concatenate([b[0], b[1], b[0]], dims[0][1][0])
    return lax.dot_general(left, right, dims, preferred_element_type=F32)


def every(start, count, stride):
    return pl.ds(start, count, stride=stride)


def swap_halves(x):
    return pltpu.roll(x, 64, 1)


def lower():
    return lax.broadcasted_iota(jnp.int32, (192, 128), 1) < 64


def thirds(ref):
    return ref[every(0, 192, 3), :], ref[every(1, 192, 3), :], ref[every(2, 192, 3), :]


def put_thirds(ref, parts):
    for i in range(3):
        ref[every(i, 192, 3), :] = parts[i]


def whole(ref):
    return jnp.concatenate([ref[i] for i in range(ref.shape[0])], 1)


def put_whole(ref, x):
    for i in range(ref.shape[0]):
        ref[i] = x[:, 128 * i : 128 * i + 128]


def put_half(dst, parts):
    a, b, c = parts
    low = lower()
    zero = jnp.zeros((192, 128), F32)
    even, odd = every(0, 192, 2), every(1, 192, 2)
    cs = swap_halves(c)
    dst[0, even, :] = a
    dst[1, even, :] = jnp.where(low, b, zero)
    dst[0, odd, :] = jnp.where(low, swap_halves(b), cs)
    dst[1, odd, :] = jnp.where(low, cs, zero)


def get_half(src):
    low = lower()
    even, odd = every(0, 192, 2), every(1, 192, 2)
    os = swap_halves(src[0, odd, :])
    return (
        src[0, even, :],
        jnp.where(low, src[1, even, :], os),
        jnp.where(low, os, swap_halves(src[1, odd, :])),
    )


def put_full(dst, first, second):
    a0, b0, c0 = thirds(first)
    a1, b1, c1 = thirds(second)
    low = lower()
    even, odd = every(0, 192, 2), every(1, 192, 2)
    a1s, c0s = swap_halves(a1), swap_halves(c0)
    dst[0, even, :] = a0
    dst[1, even, :] = jnp.where(low, b0, a1s)
    dst[2, even, :] = jnp.where(low, a1s, swap_halves(b1))
    dst[0, odd, :] = jnp.where(low, swap_halves(b0), c0s)
    dst[1, odd, :] = jnp.where(low, c0s, b1)
    dst[2, odd, :] = c1


def flat_full(src, first, second):
    low = lower()
    even, odd = every(0, 192, 2), every(1, 192, 2)
    e0, e1, e2 = (src[i, even, :] for i in range(3))
    o0, o1, o2 = (src[i, odd, :] for i in range(3))
    o0s, e2s = swap_halves(o0), swap_halves(e2)
    put_thirds(first, (e0, jnp.where(low, e1, o0s), jnp.where(low, o0s, swap_halves(o1))))
    put_thirds(second, (jnp.where(low, swap_halves(e1), e2s), jnp.where(low, e2s, o1), o2))


def nth(i):
    return jnp.where((i & 1) == 1, (i + 1) // 2, 8 - i // 2)


def kernel(
    g_in, m1_in, m2_in, ls_in, rs_in, lb_in, rb_in,
    upd_out, nm_out, nv_out, nl_out, nr_out, ql_out, qr_out,
    gs, hop, gbuf, gfull, sraw, lraw, rraw, m1, m2, sfull, qfull, rhalf, work, zbuf, xbuf,
    wp, wr, us, back, pack, ub, upd, nflat, xflat,
    qlh, qll, qth, qtl, qoh, qol,
    lsem, gsem, ssend, srecv, p1s, p1r, p2s, p2r, own, xs, xr, ws, wrv, r1s, r1r, r2s, r2r, ts, tr, osem,
):
    me, t = lax.axis_index("shard"), lax.axis_index("tensor")
    h = me & 1
    chip = me // 2
    cy, cz = chip // 8, chip & 7
    first = h == 0
    a = jnp.where(first, cy, cz)
    b = jnp.where(first, cz, cy)

    def along_one(p):
        return 2 * jnp.where(first, p * 8 + cz, cy * 8 + p) + h

    def along_two(q):
        return 2 * jnp.where(first, cy * 8 + q, q * 8 + cz) + h

    partner = me + 1 - 2 * h

    def remote(src, dst, send, recv, device):
        return pltpu.make_async_remote_copy(
            src_ref=src, dst_ref=dst, send_sem=send, recv_sem=recv, device_id=(device, t), device_id_type=MESH
        )

    barrier = pltpu.get_barrier_semaphore()

    def greet(device):
        pl.semaphore_signal(barrier, inc=1, device_id=(device, t), device_id_type=MESH)

    def greetings(i, carry):
        greet(along_one((a + i) & 7))
        greet(along_two((b + i) & 7))
        return carry

    lax.fori_loop(1, 8, greetings, 0)
    greet(partner)

    def stage(p, carry):
        @pl.when(first)
        def _():
            pltpu.make_async_copy(g_in.at[:, p, :, :], gs.at[p], gsem).start()

        @pl.when(jnp.logical_not(first))
        def _():
            pltpu.make_async_copy(g_in.at[:, :, p, :], gs.at[p], gsem).start()

        return carry

    lax.fori_loop(0, 8, stage, 0)

    @pl.when(first)
    def _():
        pltpu.make_async_copy(ls_in, sraw.at[0], lsem.at[0]).start()

    @pl.when(jnp.logical_not(first))
    def _():
        pltpu.make_async_copy(rs_in, sraw.at[1], lsem.at[0]).start()

    loads = [
        pltpu.make_async_copy(ls_in, sraw.at[h], lsem.at[0]),
        pltpu.make_async_copy(lb_in, lraw.at[h], lsem.at[1]),
        pltpu.make_async_copy(rb_in, rraw.at[h], lsem.at[2]),
        pltpu.make_async_copy(m1_in, m1, lsem.at[3]),
        pltpu.make_async_copy(m2_in, m2, lsem.at[4]),
    ]
    for load in loads[1:]:
        load.start()
    pltpu.make_async_copy(gs, gs, gsem).wait()
    pl.semaphore_wait(barrier, 15)

    def hop_one(i):
        p = (a + i) & 7
        return remote(gs.at[p], hop.at[a], p1s.at[p], p1r.at[a], along_one(p))

    def start_one(i, carry):
        hop_one(nth(8 - i)).start()
        return carry

    lax.fori_loop(1, 8, start_one, 0)

    def forward(src, s):
        def send(i, carry):
            q = (b + nth(8 - i)) & 7
            remote(
                src.at[:, pl.ds(q, 1), :], gbuf.at[h, b, :, pl.ds(s, 1), :], p2s.at[q], p2r.at[b], along_two(q)
            ).start()
            return carry

        lax.fori_loop(1, 8, send, 0)
        pltpu.make_async_copy(src.at[:, pl.ds(b, 1), :], gbuf.at[h, b, :, pl.ds(s, 1), :], own).start()

    forward(gs.at[a], a)

    swaps = [
        remote(lb_in, lraw.at[h], ssend.at[1], srecv.at[1], partner),
        remote(rb_in, rraw.at[h], ssend.at[2], srecv.at[2], partner),
    ]
    for copy in swaps:
        copy.start()

    @pl.when(first)
    def _():
        remote(rs_in, sraw.at[h], ssend.at[0], srecv.at[0], partner).start()

    @pl.when(jnp.logical_not(first))
    def _():
        remote(ls_in, sraw.at[h], ssend.at[0], srecv.at[0], partner).start()

    swap_stat = remote(ls_in, sraw.at[h], ssend.at[0], srecv.at[0], partner)

    def relay(i, carry):
        s = (a + nth(i)) & 7
        remote(gs.at[s], hop.at[s], p1s.at[s], p1r.at[s], along_one(s)).wait_recv()
        forward(hop.at[s], s)
        return carry

    lax.fori_loop(1, 8, relay, 0)

    for load in loads:
        load.wait()
    for copy in swaps:
        copy.wait()
    swap_stat.wait()
    put_full(qfull.at[0], lraw.at[0], lraw.at[1])
    put_full(qfull.at[1], rraw.at[0], rraw.at[1])
    put_full(sfull, sraw.at[0], sraw.at[1])
    put_half(rhalf.at[0], thirds(rraw.at[0]))
    put_half(rhalf.at[1], thirds(rraw.at[1]))
    left = whole(qfull.at[0])
    qlh[...], qll[...] = split(left)
    qth[...], qtl[...] = split(left.T)
    qoh[...], qol[...] = split(whole(qfull.at[h]))

    pltpu.make_async_copy(gbuf.at[0, 0], gbuf.at[0, 0], own).wait()

    def cross(k):
        return remote(gbuf.at[h, k], gbuf.at[h, k], xs.at[k], xr.at[k], partner)

    cross(b).start()

    def pass_on(i, carry):
        k = (b + nth(i)) & 7
        remote(gbuf.at[h, k], gbuf.at[h, k], p2s.at[k], p2r.at[k], along_two(k)).wait_recv()
        cross(k).start()
        return carry

    lax.fori_loop(1, 8, pass_on, 0)

    def crossed(k, carry):
        remote(gbuf.at[1 - h, k], gbuf.at[1 - h, k], xs.at[k], xr.at[k], partner).wait_recv()
        return carry

    lax.fori_loop(0, 8, crossed, 0)
    for k in range(8):
        for r in range(3):
            for c in range(3):
                lanes = pl.ds(128 * c, 128)
                gfull[c, every(6 * k + r, 8, 48), :] = gbuf[0, k, r, :, lanes]
                gfull[c, every(48 * k + 3 + r, 8, 6), :] = gbuf[1, k, r, :, lanes]
    grad = whole(gfull)

    rot = dot((qth[...], qtl[...]), split(dot(split(grad), split(whole(rhalf.at[h])))))
    put_whole(work, rot)
    parts = []
    for i, turned in enumerate(get_half(work)):
        rows = every(i, 192, 3)
        new_first = BETA_ONE * m1[rows, :] + (1.0 - BETA_ONE) * turned
        new_second = BETA_TWO * m2[rows, :] + (1.0 - BETA_TWO) * turned * turned
        m1[rows, :] = new_first
        m2[rows, :] = new_second
        parts.append(new_first / (jnp.sqrt(new_second) + ADAM_EPS))
    stores = [
        pltpu.make_async_copy(m1, nm_out, osem.at[0]),
        pltpu.make_async_copy(m2, nv_out, osem.at[1]),
    ]
    for store in stores:
        store.start()
    put_half(work, parts)
    put_whole(work, dot((qlh[...], qll[...]), split(whole(work))))
    for p in range(8):
        for r in range(3):
            rows = pl.ds((3 * p + r) * 8, 8)
            for c in range(2):
                lanes = pl.ds(128 * c, 128)
                wp[0, rows, lanes] = work[c, every(48 * p + r, 8, 6), :]
                wp[1, rows, lanes] = work[c, every(6 * p + 3 + r, 8, 48), :]
    swap_w = remote(wp.at[1 - h], wr, ws, wrv, partner)
    swap_w.start()

    @pl.when(first)
    def _():
        zbuf[...] = grad

    @pl.when(jnp.logical_not(first))
    def _():
        zbuf[...] = grad.T

    z = split(zbuf[...])
    stat = 0.5 * whole(sfull) + 0.5 * dot(z, z, NT)

    swap_w.wait()
    mine = dot(split(wp[h]), split(whole(rhalf.at[h])), NT)
    us[...] = (mine + dot(split(wr[...]), split(whole(rhalf.at[1 - h])), NT)).reshape(8, 3, 8, B)

    def back_one(i):
        p = (a + i) & 7
        return remote(us.at[p], back.at[a], r1s.at[p], r1r.at[a], along_one(p))

    def start_back(i, carry):
        back_one(nth(8 - i)).start()
        return carry

    lax.fori_loop(1, 8, start_back, 0)
    keep = pltpu.make_async_copy(us.at[a], back.at[a], own)
    keep.start()

    put_whole(sfull, stat)
    power = dot(split(stat), (qoh[...], qol[...]))
    scale = 1.0 / jnp.sqrt(jnp.sum(power * power) + NORM_EPS)
    x = power * scale
    flat_full(sfull, nflat.at[0], nflat.at[1])

    def halves_out(flat, left_out, right_out, sem, send, recv):
        @pl.when(first)
        def _():
            pltpu.make_async_copy(flat.at[0], left_out, sem).start()
            remote(flat.at[1], left_out, send, recv, partner).start()

        @pl.when(jnp.logical_not(first))
        def _():
            pltpu.make_async_copy(flat.at[1], right_out, sem).start()
            remote(flat.at[0], right_out, send, recv, partner).start()

    def halves_wait(flat, left_out, right_out, sem, send, recv):
        pltpu.make_async_copy(flat.at[0], left_out, sem).wait()

        @pl.when(first)
        def _():
            remote(flat.at[1], right_out, send, recv, partner).wait()

        @pl.when(jnp.logical_not(first))
        def _():
            remote(flat.at[0], left_out, send, recv, partner).wait()

    halves_out(nflat, nl_out, nr_out, osem.at[2], ts.at[0], tr.at[0])

    def quintic(x):
        parts = split(x)
        gram = dot(parts, parts, NT)
        g = split(gram)
        poly = CUBIC_COEFF * gram + QUINTIC_COEFF * dot(g, g)
        return LINEAR_COEFF * x + dot(split(poly), parts)

    x = quintic(quintic(x))

    def landed(i, carry):
        s = (a + i) & 7
        remote(us.at[s], back.at[s], r1s.at[s], r1r.at[s], along_one(s)).wait()
        return carry

    lax.fori_loop(1, 8, landed, 0)
    keep.wait()
    for s in range(8):
        for r in range(3):
            for c in range(3):
                pack[c, every(r * 8 + s, 8, 24), :] = back[s, r, :, 128 * c : 128 * c + 128]

    def back_two(i):
        q = (b + i) & 7
        return remote(pack.at[:, pl.ds(pl.multiple_of(q * 24, 8), 24), :], ub.at[b], r2s.at[q], r2r.at[b], along_two(q))

    def start_two(i, carry):
        back_two(nth(8 - i)).start()
        return carry

    lax.fori_loop(1, 8, start_two, 0)
    keep_two = pltpu.make_async_copy(pack.at[:, pl.ds(pl.multiple_of(b * 24, 8), 24), :], ub.at[b], own)
    keep_two.start()

    x = quintic(quintic(quintic(x)))
    put_whole(xbuf, x)
    flat_full(xbuf, xflat.at[0], xflat.at[1])
    halves_out(xflat, ql_out, qr_out, osem.at[3], ts.at[1], tr.at[1])

    def arrived(i, carry):
        q = (b + i) & 7
        remote(
            pack.at[:, pl.ds(pl.multiple_of(q * 24, 8), 24), :], ub.at[q], r2s.at[q], r2r.at[q], along_two(q)
        ).wait()
        return carry

    lax.fori_loop(1, 8, arrived, 0)
    keep_two.wait()

    @pl.when(first)
    def _():
        for k in range(8):
            for r in range(3):
                for c in range(3):
                    upd[c, every(64 * r + k, 8, 8), :] = ub[k, c, pl.ds(8 * r, 8), :]

    @pl.when(jnp.logical_not(first))
    def _():
        for k in range(8):
            for r in range(3):
                for c in range(3):
                    upd[c, pl.ds(64 * r + 8 * k, 8), :] = ub[k, c, pl.ds(8 * r, 8), :]

    lasts = [
        pltpu.make_async_copy(upd.at[c], upd_out.at[:, pl.ds(128 * c, 128)], osem.at[4 + c]) for c in range(3)
    ]
    for last in lasts:
        last.start()

    def sent(i, carry):
        p = (a + i) & 7
        q = (b + i) & 7
        remote(gs.at[p], hop.at[a], p1s.at[p], p1r.at[a], along_one(p)).wait_send()
        remote(gbuf.at[h, q], gbuf.at[h, q], p2s.at[q], p2r.at[q], along_two(q)).wait_send()
        return carry

    lax.fori_loop(1, 8, sent, 0)

    def sent_cross(k, carry):
        cross(k).wait_send()
        return carry

    lax.fori_loop(0, 8, sent_cross, 0)
    for store in stores:
        store.wait()
    halves_wait(nflat, nl_out, nr_out, osem.at[2], ts.at[0], tr.at[0])
    halves_wait(xflat, ql_out, qr_out, osem.at[3], ts.at[1], tr.at[1])
    for last in lasts:
        last.wait()


def step(grads, *flats):
    tiles = (LINES, 128)
    square = (B, B)
    dma = pltpu.SemaphoreType.DMA
    scratch = [
        pltpu.VMEM((8, 3, 8, B), F32),
        pltpu.VMEM((8, 3, 8, B), F32),
        pltpu.VMEM((2, 8, 3, 8, B), F32),
        pltpu.VMEM((3, B, 128), F32),
        pltpu.VMEM((2, *tiles), F32),
        pltpu.VMEM((2, *tiles), F32),
        pltpu.VMEM((2, *tiles), F32),
        pltpu.VMEM(tiles, F32),
        pltpu.VMEM(tiles, F32),
        pltpu.VMEM((3, B, 128), F32),
        pltpu.VMEM((2, 3, B, 128), F32),
        pltpu.VMEM((2, 2, B, 128), F32),
        pltpu.VMEM((2, B, 128), F32),
        pltpu.VMEM(square, F32),
        pltpu.VMEM((3, B, 128), F32),
        pltpu.VMEM((2, 192, 256), F32),
        pltpu.VMEM((192, 256), F32),
        pltpu.VMEM((8, 3, 8, B), F32),
        pltpu.VMEM((8, 3, 8, B), F32),
        pltpu.VMEM((3, 192, 128), F32),
        pltpu.VMEM((8, 3, 24, 128), F32),
        pltpu.VMEM((3, 192, 128), F32),
        pltpu.VMEM((2, *tiles), F32),
        pltpu.VMEM((2, *tiles), F32),
        *[pltpu.VMEM(square, BF16)] * 6,
        dma((5,)),
        dma,
        dma((3,)),
        dma((3,)),
        *[dma((8,))] * 4,
        dma,
        *[dma((8,))] * 2,
        *[dma] * 2,
        *[dma((8,))] * 4,
        *[dma((2,))] * 2,
        dma((7,)),
    ]
    anywhere = pl.BlockSpec(memory_space=pl.ANY)
    flat = jax.ShapeDtypeStruct(tiles, F32)
    outs = pl.pallas_call(
        kernel,
        out_shape=(jax.ShapeDtypeStruct((192, B), F32), *[flat] * 6),
        in_specs=[anywhere] * 7,
        out_specs=(anywhere,) * 7,
        scratch_shapes=scratch,
        compiler_params=pltpu.CompilerParams(collective_id=0, has_side_effects=True, vmem_limit_bytes=60 << 20),
        name="soap_step",
    )(grads.transpose(1, 0, 2).reshape(3, 8, 8, B), *[x.reshape(tiles) for x in flats])
    return (outs[0].reshape(3, 64, B).transpose(1, 0, 2), *[x.reshape(1, -1) for x in outs[1:]])


def solution(mesh):
    specs = (P("tensor", "shard", None), *[P(("tensor", "shard"), None)] * 6)
    return jax.shard_map(step, mesh=mesh, in_specs=specs, out_specs=specs, check_vma=False)
```

```python
import jax
import jax.numpy as jnp
from jax import lax
from jax.experimental import pallas as pl
from jax.experimental.pallas import tpu as pltpu
from jax.sharding import PartitionSpec as P

NS_ITERS = 5
BETA_ONE = 0.9
BETA_TWO = 0.95
ADAM_EPS = 1e-08
NORM_EPS = 1e-06
LINEAR_COEFF = 3.4445
CUBIC_COEFF = -4.775
QUINTIC_COEFF = 2.0315

B = 384
LINES = 576
VMEM_BYTES = 30 << 20
MESH = pl.DeviceIdType.MESH
F32 = jnp.float32
BF16 = jnp.bfloat16
NN = (((1,), (0,)), ((), ()))
NT = (((1,), (1,)), ((), ()))


def split(x):
    high = x.astype(BF16)
    return high, (x - high.astype(F32)).astype(BF16)


def dot(a, b, dims=NN):
    left = jnp.concatenate([a[0], a[0], a[1]], dims[0][0][0])
    right = jnp.concatenate([b[0], b[1], b[0]], dims[0][1][0])
    return lax.dot_general(left, right, dims, preferred_element_type=F32)


def every(start, count, stride):
    return pl.ds(start, count, stride=stride)


def swap_halves(x):
    return pltpu.roll(x, 64, 1)


def lower():
    return lax.broadcasted_iota(jnp.int32, (192, 128), 1) < 64


def thirds(ref):
    return ref[every(0, 192, 3), :], ref[every(1, 192, 3), :], ref[every(2, 192, 3), :]


def put_thirds(ref, parts):
    for i in range(3):
        ref[every(i, 192, 3), :] = parts[i]


def whole(ref):
    return jnp.concatenate([ref[i] for i in range(ref.shape[0])], 1)


def put_whole(ref, x):
    for i in range(ref.shape[0]):
        ref[i] = x[:, 128 * i : 128 * i + 128]


def put_half(dst, parts):
    a, b, c = parts
    low = lower()
    zero = jnp.zeros((192, 128), F32)
    even, odd = every(0, 192, 2), every(1, 192, 2)
    cs = swap_halves(c)
    dst[0, even, :] = a
    dst[1, even, :] = jnp.where(low, b, zero)
    dst[0, odd, :] = jnp.where(low, swap_halves(b), cs)
    dst[1, odd, :] = jnp.where(low, cs, zero)


def get_half(src):
    low = lower()
    even, odd = every(0, 192, 2), every(1, 192, 2)
    os = swap_halves(src[0, odd, :])
    return (
        src[0, even, :],
        jnp.where(low, src[1, even, :], os),
        jnp.where(low, os, swap_halves(src[1, odd, :])),
    )


def put_full(dst, first, second):
    a0, b0, c0 = thirds(first)
    a1, b1, c1 = thirds(second)
    low = lower()
    even, odd = every(0, 192, 2), every(1, 192, 2)
    a1s, c0s = swap_halves(a1), swap_halves(c0)
    dst[0, even, :] = a0
    dst[1, even, :] = jnp.where(low, b0, a1s)
    dst[2, even, :] = jnp.where(low, a1s, swap_halves(b1))
    dst[0, odd, :] = jnp.where(low, swap_halves(b0), c0s)
    dst[1, odd, :] = jnp.where(low, c0s, b1)
    dst[2, odd, :] = c1


def flat_full(src, first, second):
    low = lower()
    even, odd = every(0, 192, 2), every(1, 192, 2)
    e0, e1, e2 = (src[i, even, :] for i in range(3))
    o0, o1, o2 = (src[i, odd, :] for i in range(3))
    o0s, e2s = swap_halves(o0), swap_halves(e2)
    put_thirds(first, (e0, jnp.where(low, e1, o0s), jnp.where(low, o0s, swap_halves(o1))))
    put_thirds(second, (jnp.where(low, swap_halves(e1), e2s), jnp.where(low, e2s, o1), o2))


def nth(i):
    return jnp.where((i & 1) == 1, (i + 1) // 2, 8 - i // 2)


def kernel(
    g_in, m1_in, m2_in, ls_in, rs_in, lb_in, rb_in,
    upd_out, nm_out, nv_out, nl_out, nr_out, ql_out, qr_out,
    gs, hop, gbuf, gfull, sraw, lraw, rraw, m1, m2, sfull, qfull, rhalf, work, zbuf, xbuf,
    wp, wr, us, back, pack, ub, upd, nflat, xflat,
    qlh, qll, qth, qtl, qoh, qol,
    lsem, gsem, ssend, srecv, p1s, p1r, p2s, p2r, own, xs, xr, ws, wrv, r1s, r1r, r2s, r2r, ts, tr, osem,
):
    me, t = lax.axis_index("shard"), lax.axis_index("tensor")
    h = me & 1
    chip = me // 2
    cy, cz = chip // 8, chip & 7
    first = h == 0
    a = jnp.where(first, cy, cz)
    b = jnp.where(first, cz, cy)

    def along_one(p):
        return 2 * jnp.where(first, p * 8 + cz, cy * 8 + p) + h

    def along_two(q):
        return 2 * jnp.where(first, cy * 8 + q, q * 8 + cz) + h

    partner = me + 1 - 2 * h

    def remote(src, dst, send, recv, device):
        return pltpu.make_async_remote_copy(
            src_ref=src, dst_ref=dst, send_sem=send, recv_sem=recv, device_id=(device, t), device_id_type=MESH
        )

    barrier = pltpu.get_barrier_semaphore()

    def greet(device):
        pl.semaphore_signal(barrier, inc=1, device_id=(device, t), device_id_type=MESH)

    def greetings(i, carry):
        greet(along_one((a + i) & 7))
        greet(along_two((b + i) & 7))
        return carry

    lax.fori_loop(1, 8, greetings, 0)
    greet(partner)

    def stage(p, carry):
        @pl.when(first)
        def _():
            pltpu.make_async_copy(g_in.at[:, p, :, :], gs.at[p], gsem).start()

        @pl.when(jnp.logical_not(first))
        def _():
            pltpu.make_async_copy(g_in.at[:, :, p, :], gs.at[p], gsem).start()

        return carry

    lax.fori_loop(0, 8, stage, 0)

    @pl.when(first)
    def _():
        pltpu.make_async_copy(ls_in, sraw.at[0], lsem.at[0]).start()

    @pl.when(jnp.logical_not(first))
    def _():
        pltpu.make_async_copy(rs_in, sraw.at[1], lsem.at[0]).start()

    loads = [
        pltpu.make_async_copy(ls_in, sraw.at[h], lsem.at[0]),
        pltpu.make_async_copy(lb_in, lraw.at[h], lsem.at[1]),
        pltpu.make_async_copy(rb_in, rraw.at[h], lsem.at[2]),
        pltpu.make_async_copy(m1_in, m1, lsem.at[3]),
        pltpu.make_async_copy(m2_in, m2, lsem.at[4]),
    ]
    for load in loads[1:]:
        load.start()
    pltpu.make_async_copy(gs, gs, gsem).wait()
    pl.semaphore_wait(barrier, 15)

    def hop_one(i):
        p = (a + i) & 7
        return remote(gs.at[p], hop.at[a], p1s.at[p], p1r.at[a], along_one(p))

    def start_one(i, carry):
        hop_one(nth(8 - i)).start()
        return carry

    lax.fori_loop(1, 8, start_one, 0)

    def forward(src, s):
        def send(i, carry):
            q = (b + nth(8 - i)) & 7
            remote(
                src.at[:, pl.ds(q, 1), :], gbuf.at[h, b, :, pl.ds(s, 1), :], p2s.at[q], p2r.at[b], along_two(q)
            ).start()
            return carry

        lax.fori_loop(1, 8, send, 0)
        pltpu.make_async_copy(src.at[:, pl.ds(b, 1), :], gbuf.at[h, b, :, pl.ds(s, 1), :], own).start()

    forward(gs.at[a], a)

    swaps = [
        remote(lb_in, lraw.at[h], ssend.at[1], srecv.at[1], partner),
        remote(rb_in, rraw.at[h], ssend.at[2], srecv.at[2], partner),
    ]
    for copy in swaps:
        copy.start()

    @pl.when(first)
    def _():
        remote(rs_in, sraw.at[h], ssend.at[0], srecv.at[0], partner).start()

    @pl.when(jnp.logical_not(first))
    def _():
        remote(ls_in, sraw.at[h], ssend.at[0], srecv.at[0], partner).start()

    swap_stat = remote(ls_in, sraw.at[h], ssend.at[0], srecv.at[0], partner)

    def relay(i, carry):
        s = (a + nth(i)) & 7
        remote(gs.at[s], hop.at[s], p1s.at[s], p1r.at[s], along_one(s)).wait_recv()
        forward(hop.at[s], s)
        return carry

    lax.fori_loop(1, 8, relay, 0)

    for load in loads:
        load.wait()
    for copy in swaps:
        copy.wait()
    swap_stat.wait()
    put_full(qfull.at[0], lraw.at[0], lraw.at[1])
    put_full(qfull.at[1], rraw.at[0], rraw.at[1])
    put_full(sfull, sraw.at[0], sraw.at[1])
    put_half(rhalf.at[0], thirds(rraw.at[0]))
    put_half(rhalf.at[1], thirds(rraw.at[1]))
    left = whole(qfull.at[0])
    qlh[...], qll[...] = split(left)
    qth[...], qtl[...] = split(left.T)
    qoh[...], qol[...] = split(whole(qfull.at[h]))

    pltpu.make_async_copy(gbuf.at[0, 0], gbuf.at[0, 0], own).wait()

    def cross(k):
        return remote(gbuf.at[h, k], gbuf.at[h, k], xs.at[k], xr.at[k], partner)

    cross(b).start()

    def pass_on(i, carry):
        k = (b + nth(i)) & 7
        remote(gbuf.at[h, k], gbuf.at[h, k], p2s.at[k], p2r.at[k], along_two(k)).wait_recv()
        cross(k).start()
        return carry

    lax.fori_loop(1, 8, pass_on, 0)

    def crossed(k, carry):
        remote(gbuf.at[1 - h, k], gbuf.at[1 - h, k], xs.at[k], xr.at[k], partner).wait_recv()
        return carry

    lax.fori_loop(0, 8, crossed, 0)
    for k in range(8):
        for r in range(3):
            for c in range(3):
                lanes = pl.ds(128 * c, 128)
                gfull[c, every(6 * k + r, 8, 48), :] = gbuf[0, k, r, :, lanes]
                gfull[c, every(48 * k + 3 + r, 8, 6), :] = gbuf[1, k, r, :, lanes]
    grad = whole(gfull)

    rot = dot((qth[...], qtl[...]), split(dot(split(grad), split(whole(rhalf.at[h])))))
    put_whole(work, rot)
    parts = []
    for i, turned in enumerate(get_half(work)):
        rows = every(i, 192, 3)
        new_first = BETA_ONE * m1[rows, :] + (1.0 - BETA_ONE) * turned
        new_second = BETA_TWO * m2[rows, :] + (1.0 - BETA_TWO) * turned * turned
        m1[rows, :] = new_first
        m2[rows, :] = new_second
        parts.append(new_first / (jnp.sqrt(new_second) + ADAM_EPS))
    stores = [
        pltpu.make_async_copy(m1, nm_out, osem.at[0]),
        pltpu.make_async_copy(m2, nv_out, osem.at[1]),
    ]
    for store in stores:
        store.start()
    put_half(work, parts)
    put_whole(work, dot((qlh[...], qll[...]), split(whole(work))))
    for p in range(8):
        for r in range(3):
            rows = pl.ds((3 * p + r) * 8, 8)
            for c in range(2):
                lanes = pl.ds(128 * c, 128)
                wp[0, rows, lanes] = work[c, every(48 * p + r, 8, 6), :]
                wp[1, rows, lanes] = work[c, every(6 * p + 3 + r, 8, 48), :]
    swap_w = remote(wp.at[1 - h], wr, ws, wrv, partner)
    swap_w.start()

    @pl.when(first)
    def _():
        zbuf[...] = grad

    @pl.when(jnp.logical_not(first))
    def _():
        zbuf[...] = grad.T

    z = split(zbuf[...])
    stat = 0.5 * whole(sfull) + 0.5 * dot(z, z, NT)

    swap_w.wait()
    mine = dot(split(wp[h]), split(whole(rhalf.at[h])), NT)
    us[...] = (mine + dot(split(wr[...]), split(whole(rhalf.at[1 - h])), NT)).reshape(8, 3, 8, B)

    def back_one(i):
        p = (a + i) & 7
        return remote(us.at[p], back.at[a], r1s.at[p], r1r.at[a], along_one(p))

    def start_back(i, carry):
        back_one(nth(8 - i)).start()
        return carry

    lax.fori_loop(1, 8, start_back, 0)
    keep = pltpu.make_async_copy(us.at[a], back.at[a], own)
    keep.start()

    put_whole(sfull, stat)
    power = dot(split(stat), (qoh[...], qol[...]))
    scale = 1.0 / jnp.sqrt(jnp.sum(power * power) + NORM_EPS)
    x = power * scale
    flat_full(sfull, nflat.at[0], nflat.at[1])

    def halves_out(flat, left_out, right_out, sem, send, recv):
        @pl.when(first)
        def _():
            pltpu.make_async_copy(flat.at[0], left_out, sem).start()
            remote(flat.at[1], left_out, send, recv, partner).start()

        @pl.when(jnp.logical_not(first))
        def _():
            pltpu.make_async_copy(flat.at[1], right_out, sem).start()
            remote(flat.at[0], right_out, send, recv, partner).start()

    def halves_wait(flat, left_out, right_out, sem, send, recv):
        pltpu.make_async_copy(flat.at[0], left_out, sem).wait()

        @pl.when(first)
        def _():
            remote(flat.at[1], right_out, send, recv, partner).wait()

        @pl.when(jnp.logical_not(first))
        def _():
            remote(flat.at[0], left_out, send, recv, partner).wait()

    halves_out(nflat, nl_out, nr_out, osem.at[2], ts.at[0], tr.at[0])

    def quintic(x):
        parts = split(x)
        gram = dot(parts, parts, NT)
        g = split(gram)
        poly = CUBIC_COEFF * gram + QUINTIC_COEFF * dot(g, g)
        return LINEAR_COEFF * x + dot(split(poly), parts)

    x = quintic(quintic(x))

    def landed(i, carry):
        s = (a + i) & 7
        remote(us.at[s], back.at[s], r1s.at[s], r1r.at[s], along_one(s)).wait()
        return carry

    lax.fori_loop(1, 8, landed, 0)
    keep.wait()
    for s in range(8):
        for r in range(3):
            for c in range(3):
                pack[c, every(r * 8 + s, 8, 24), :] = back[s, r, :, 128 * c : 128 * c + 128]

    def back_two(i):
        q = (b + i) & 7
        return remote(pack.at[:, pl.ds(pl.multiple_of(q * 24, 8), 24), :], ub.at[b], r2s.at[q], r2r.at[b], along_two(q))

    def start_two(i, carry):
        back_two(nth(8 - i)).start()
        return carry

    lax.fori_loop(1, 8, start_two, 0)
    keep_two = pltpu.make_async_copy(pack.at[:, pl.ds(pl.multiple_of(b * 24, 8), 24), :], ub.at[b], own)
    keep_two.start()

    x = quintic(quintic(quintic(x)))
    put_whole(xbuf, x)
    flat_full(xbuf, xflat.at[0], xflat.at[1])
    halves_out(xflat, ql_out, qr_out, osem.at[3], ts.at[1], tr.at[1])

    def arrived(i, carry):
        q = (b + i) & 7
        remote(
            pack.at[:, pl.ds(pl.multiple_of(q * 24, 8), 24), :], ub.at[q], r2s.at[q], r2r.at[q], along_two(q)
        ).wait()
        return carry

    lax.fori_loop(1, 8, arrived, 0)
    keep_two.wait()

    @pl.when(first)
    def _():
        for k in range(8):
            for r in range(3):
                for c in range(3):
                    upd[c, every(64 * r + k, 8, 8), :] = ub[k, c, pl.ds(8 * r, 8), :]

    @pl.when(jnp.logical_not(first))
    def _():
        for k in range(8):
            for r in range(3):
                for c in range(3):
                    upd[c, pl.ds(64 * r + 8 * k, 8), :] = ub[k, c, pl.ds(8 * r, 8), :]

    lasts = [
        pltpu.make_async_copy(upd.at[c], upd_out.at[:, pl.ds(128 * c, 128)], osem.at[4 + c]) for c in range(3)
    ]
    for last in lasts:
        last.start()

    def sent(i, carry):
        p = (a + i) & 7
        q = (b + i) & 7
        remote(gs.at[p], hop.at[a], p1s.at[p], p1r.at[a], along_one(p)).wait_send()
        remote(gbuf.at[h, q], gbuf.at[h, q], p2s.at[q], p2r.at[q], along_two(q)).wait_send()
        return carry

    lax.fori_loop(1, 8, sent, 0)

    def sent_cross(k, carry):
        cross(k).wait_send()
        return carry

    lax.fori_loop(0, 8, sent_cross, 0)
    for store in stores:
        store.wait()
    halves_wait(nflat, nl_out, nr_out, osem.at[2], ts.at[0], tr.at[0])
    halves_wait(xflat, ql_out, qr_out, osem.at[3], ts.at[1], tr.at[1])
    for last in lasts:
        last.wait()


def hand_out(*refs):
    copies = [pltpu.make_async_copy(refs[i], refs[7 + i], refs[14].at[i]) for i in range(7)]
    for copy in copies:
        copy.start()
    for copy in copies:
        copy.wait()


def step(grads, *flats):
    tiles = (LINES, 128)
    square = (B, B)
    dma = pltpu.SemaphoreType.DMA
    scratch = [
        pltpu.VMEM((8, 3, 8, B), F32),
        pltpu.VMEM((8, 3, 8, B), F32),
        pltpu.VMEM((2, 8, 3, 8, B), F32),
        pltpu.VMEM((3, B, 128), F32),
        pltpu.VMEM((2, *tiles), F32),
        pltpu.VMEM((2, *tiles), F32),
        pltpu.VMEM((2, *tiles), F32),
        pltpu.VMEM(tiles, F32),
        pltpu.VMEM(tiles, F32),
        pltpu.VMEM((3, B, 128), F32),
        pltpu.VMEM((2, 3, B, 128), F32),
        pltpu.VMEM((2, 2, B, 128), F32),
        pltpu.VMEM((2, B, 128), F32),
        pltpu.VMEM(square, F32),
        pltpu.VMEM((3, B, 128), F32),
        pltpu.VMEM((2, 192, 256), F32),
        pltpu.VMEM((192, 256), F32),
        pltpu.VMEM((8, 3, 8, B), F32),
        pltpu.VMEM((8, 3, 8, B), F32),
        pltpu.VMEM((3, 192, 128), F32),
        pltpu.VMEM((8, 3, 24, 128), F32),
        pltpu.VMEM((3, 192, 128), F32),
        pltpu.VMEM((2, *tiles), F32),
        pltpu.VMEM((2, *tiles), F32),
        *[pltpu.VMEM(square, BF16)] * 6,
        dma((5,)),
        dma,
        dma((3,)),
        dma((3,)),
        *[dma((8,))] * 4,
        dma,
        *[dma((8,))] * 2,
        *[dma] * 2,
        *[dma((8,))] * 4,
        *[dma((2,))] * 2,
        dma((7,)),
    ]
    inside = pl.BlockSpec(memory_space=pltpu.VMEM)
    outside = pl.BlockSpec(memory_space=pltpu.HBM)
    shapes = (jax.ShapeDtypeStruct((192, B), F32), *[jax.ShapeDtypeStruct(tiles, F32)] * 6)
    held = pl.pallas_call(
        kernel,
        out_shape=shapes,
        in_specs=[outside] * 7,
        out_specs=(inside,) * 7,
        scratch_shapes=scratch,
        compiler_params=pltpu.CompilerParams(collective_id=0, has_side_effects=True, vmem_limit_bytes=VMEM_BYTES),
        name="soap_step",
    )(*[pltpu.with_memory_space_constraint(x, pltpu.HBM) for x in (grads.transpose(1, 0, 2).reshape(3, 8, 8, B), *[x.reshape(tiles) for x in flats])])
    outs = pl.pallas_call(
        hand_out,
        out_shape=shapes,
        in_specs=[inside] * 7,
        out_specs=(outside,) * 7,
        scratch_shapes=[dma((7,))],
        compiler_params=pltpu.CompilerParams(vmem_limit_bytes=VMEM_BYTES),
        name="hand_out",
    )(*held)
    return (outs[0].reshape(3, 64, B).transpose(1, 0, 2), *[x.reshape(1, -1) for x in outs[1:]])


def solution(mesh):
    specs = (P("tensor", "shard", None), *[P(("tensor", "shard"), None)] * 6)
    return jax.shard_map(step, mesh=mesh, in_specs=specs, out_specs=specs, check_vma=False)
```

```python
import jax
import jax.numpy as jnp
from jax import lax
from jax.experimental import pallas as pl
from jax.experimental.pallas import tpu as pltpu
from jax.sharding import PartitionSpec as P

NS_ITERS = 5
BETA_ONE = 0.9
BETA_TWO = 0.95
ADAM_EPS = 1e-08
NORM_EPS = 1e-06
LINEAR_COEFF = 3.4445
CUBIC_COEFF = -4.775
QUINTIC_COEFF = 2.0315

B = 384
LINES = 576
VMEM_BYTES = 30 << 20
MESH = pl.DeviceIdType.MESH
F32 = jnp.float32
BF16 = jnp.bfloat16
NN = (((1,), (0,)), ((), ()))
NT = (((1,), (1,)), ((), ()))


def split(x):
    high = x.astype(BF16)
    return high, (x - high.astype(F32)).astype(BF16)


def dot(a, b, dims=NN):
    left = jnp.concatenate([a[0], a[0], a[1]], dims[0][0][0])
    right = jnp.concatenate([b[0], b[1], b[0]], dims[0][1][0])
    return lax.dot_general(left, right, dims, preferred_element_type=F32)


def symmetric(a, dims):
    cut = 256
    inner = tuple(x[:cut] if dims is NT else x[:, :cut] for x in a)
    corner = dot(tuple(x[:cut] for x in a), inner, dims)
    rows = dot(tuple(x[cut:] for x in a), a, dims)
    return jnp.concatenate([jnp.concatenate([corner, rows[:, :cut].T], 1), rows], 0)


def every(start, count, stride):
    return pl.ds(start, count, stride=stride)


def swap_halves(x):
    return pltpu.roll(x, 64, 1)


def lower():
    return lax.broadcasted_iota(jnp.int32, (192, 128), 1) < 64


def thirds(ref):
    return ref[every(0, 192, 3), :], ref[every(1, 192, 3), :], ref[every(2, 192, 3), :]


def put_thirds(ref, parts):
    for i in range(3):
        ref[every(i, 192, 3), :] = parts[i]


def whole(ref):
    return jnp.concatenate([ref[i] for i in range(ref.shape[0])], 1)


def put_whole(ref, x):
    for i in range(ref.shape[0]):
        ref[i] = x[:, 128 * i : 128 * i + 128]


def put_half(dst, parts):
    a, b, c = parts
    low = lower()
    zero = jnp.zeros((192, 128), F32)
    even, odd = every(0, 192, 2), every(1, 192, 2)
    cs = swap_halves(c)
    dst[0, even, :] = a
    dst[1, even, :] = jnp.where(low, b, zero)
    dst[0, odd, :] = jnp.where(low, swap_halves(b), cs)
    dst[1, odd, :] = jnp.where(low, cs, zero)


def get_half(src):
    low = lower()
    even, odd = every(0, 192, 2), every(1, 192, 2)
    os = swap_halves(src[0, odd, :])
    return (
        src[0, even, :],
        jnp.where(low, src[1, even, :], os),
        jnp.where(low, os, swap_halves(src[1, odd, :])),
    )


def put_full(dst, first, second):
    a0, b0, c0 = thirds(first)
    a1, b1, c1 = thirds(second)
    low = lower()
    even, odd = every(0, 192, 2), every(1, 192, 2)
    a1s, c0s = swap_halves(a1), swap_halves(c0)
    dst[0, even, :] = a0
    dst[1, even, :] = jnp.where(low, b0, a1s)
    dst[2, even, :] = jnp.where(low, a1s, swap_halves(b1))
    dst[0, odd, :] = jnp.where(low, swap_halves(b0), c0s)
    dst[1, odd, :] = jnp.where(low, c0s, b1)
    dst[2, odd, :] = c1


def flat_full(src, first, second):
    low = lower()
    even, odd = every(0, 192, 2), every(1, 192, 2)
    e0, e1, e2 = (src[i, even, :] for i in range(3))
    o0, o1, o2 = (src[i, odd, :] for i in range(3))
    o0s, e2s = swap_halves(o0), swap_halves(e2)
    put_thirds(first, (e0, jnp.where(low, e1, o0s), jnp.where(low, o0s, swap_halves(o1))))
    put_thirds(second, (jnp.where(low, swap_halves(e1), e2s), jnp.where(low, e2s, o1), o2))


def nth(i):
    return jnp.where((i & 1) == 1, (i + 1) // 2, 8 - i // 2)


def kernel(
    g_in, m1_in, m2_in, ls_in, rs_in, lb_in, rb_in,
    upd_out, nm_out, nv_out, nl_out, nr_out, ql_out, qr_out,
    gs, hop, gbuf, gfull, sraw, lraw, rraw, m1, m2, sfull, qfull, rhalf, work, zhigh, zlow, xbuf,
    wp, wr, us, back, pack, ub, upd, nflat, xflat,
    qlh, qll, qth, qtl, qoh, qol,
    lsem, gsem, ssend, srecv, p1s, p1r, p2s, p2r, own, xs, xr, ws, wrv, r1s, r1r, r2s, r2r, ts, tr, osem,
):
    me, t = lax.axis_index("shard"), lax.axis_index("tensor")
    h = me & 1
    chip = me // 2
    cy, cz = chip // 8, chip & 7
    first = h == 0
    a = jnp.where(first, cy, cz)
    b = jnp.where(first, cz, cy)

    def along_one(p):
        return 2 * jnp.where(first, p * 8 + cz, cy * 8 + p) + h

    def along_two(q):
        return 2 * jnp.where(first, cy * 8 + q, q * 8 + cz) + h

    partner = me + 1 - 2 * h

    def remote(src, dst, send, recv, device):
        return pltpu.make_async_remote_copy(
            src_ref=src, dst_ref=dst, send_sem=send, recv_sem=recv, device_id=(device, t), device_id_type=MESH
        )

    barrier = pltpu.get_barrier_semaphore()

    def greet(device):
        pl.semaphore_signal(barrier, inc=1, device_id=(device, t), device_id_type=MESH)

    def greetings(i, carry):
        greet(along_one((a + i) & 7))
        greet(along_two((b + i) & 7))
        return carry

    lax.fori_loop(1, 8, greetings, 0)
    greet(partner)

    def stage(p, carry):
        @pl.when(first)
        def _():
            pltpu.make_async_copy(g_in.at[:, p, :, :], gs.at[p], gsem).start()

        @pl.when(jnp.logical_not(first))
        def _():
            pltpu.make_async_copy(g_in.at[:, :, p, :], gs.at[p], gsem).start()

        return carry

    lax.fori_loop(0, 8, stage, 0)

    @pl.when(first)
    def _():
        pltpu.make_async_copy(ls_in, sraw.at[0], lsem.at[0]).start()

    @pl.when(jnp.logical_not(first))
    def _():
        pltpu.make_async_copy(rs_in, sraw.at[1], lsem.at[0]).start()

    loads = [
        pltpu.make_async_copy(ls_in, sraw.at[h], lsem.at[0]),
        pltpu.make_async_copy(lb_in, lraw.at[h], lsem.at[1]),
        pltpu.make_async_copy(rb_in, rraw.at[h], lsem.at[2]),
        pltpu.make_async_copy(m1_in, m1, lsem.at[3]),
        pltpu.make_async_copy(m2_in, m2, lsem.at[4]),
    ]
    for load in loads[1:]:
        load.start()
    pltpu.make_async_copy(gs, gs, gsem).wait()
    pl.semaphore_wait(barrier, 15)

    def hop_one(i):
        p = (a + i) & 7
        return remote(gs.at[p], hop.at[a], p1s.at[p], p1r.at[a], along_one(p))

    def start_one(i, carry):
        hop_one(nth(8 - i)).start()
        return carry

    lax.fori_loop(1, 8, start_one, 0)

    def forward(src, s):
        def send(i, carry):
            q = (b + nth(8 - i)) & 7
            remote(
                src.at[:, pl.ds(q, 1), :], gbuf.at[h, b, :, pl.ds(s, 1), :], p2s.at[q], p2r.at[b], along_two(q)
            ).start()
            return carry

        lax.fori_loop(1, 8, send, 0)
        pltpu.make_async_copy(src.at[:, pl.ds(b, 1), :], gbuf.at[h, b, :, pl.ds(s, 1), :], own).start()

    forward(gs.at[a], a)

    swaps = [
        remote(lb_in, lraw.at[h], ssend.at[1], srecv.at[1], partner),
        remote(rb_in, rraw.at[h], ssend.at[2], srecv.at[2], partner),
    ]
    for copy in swaps:
        copy.start()

    @pl.when(first)
    def _():
        remote(rs_in, sraw.at[h], ssend.at[0], srecv.at[0], partner).start()

    @pl.when(jnp.logical_not(first))
    def _():
        remote(ls_in, sraw.at[h], ssend.at[0], srecv.at[0], partner).start()

    swap_stat = remote(ls_in, sraw.at[h], ssend.at[0], srecv.at[0], partner)

    def relay(i, carry):
        s = (a + nth(i)) & 7
        remote(gs.at[s], hop.at[s], p1s.at[s], p1r.at[s], along_one(s)).wait_recv()
        forward(hop.at[s], s)
        return carry

    lax.fori_loop(1, 8, relay, 0)

    for load in loads:
        load.wait()
    for copy in swaps:
        copy.wait()
    swap_stat.wait()
    put_full(qfull.at[0], lraw.at[0], lraw.at[1])
    put_full(qfull.at[1], rraw.at[0], rraw.at[1])
    put_full(sfull, sraw.at[0], sraw.at[1])
    put_half(rhalf.at[0], thirds(rraw.at[0]))
    put_half(rhalf.at[1], thirds(rraw.at[1]))
    left = whole(qfull.at[0])
    qlh[...], qll[...] = split(left)
    qth[...], qtl[...] = split(left.T)
    qoh[...], qol[...] = split(whole(qfull.at[h]))

    pltpu.make_async_copy(gbuf.at[0, 0], gbuf.at[0, 0], own).wait()

    def cross(k):
        return remote(gbuf.at[h, k], gbuf.at[h, k], xs.at[k], xr.at[k], partner)

    cross(b).start()

    def pass_on(i, carry):
        k = (b + nth(i)) & 7
        remote(gbuf.at[h, k], gbuf.at[h, k], p2s.at[k], p2r.at[k], along_two(k)).wait_recv()
        cross(k).start()
        return carry

    lax.fori_loop(1, 8, pass_on, 0)

    def crossed(k, carry):
        remote(gbuf.at[1 - h, k], gbuf.at[1 - h, k], xs.at[k], xr.at[k], partner).wait_recv()
        return carry

    lax.fori_loop(0, 8, crossed, 0)
    for k in range(8):
        for r in range(3):
            for c in range(3):
                lanes = pl.ds(128 * c, 128)
                gfull[c, every(6 * k + r, 8, 48), :] = gbuf[0, k, r, :, lanes]
                gfull[c, every(48 * k + 3 + r, 8, 6), :] = gbuf[1, k, r, :, lanes]
    grad_parts = split(whole(gfull))

    rot = dot((qth[...], qtl[...]), split(dot(grad_parts, split(whole(rhalf.at[h])))))
    put_whole(work, rot)
    parts = []
    for i, turned in enumerate(get_half(work)):
        rows = every(i, 192, 3)
        new_first = BETA_ONE * m1[rows, :] + (1.0 - BETA_ONE) * turned
        new_second = BETA_TWO * m2[rows, :] + (1.0 - BETA_TWO) * turned * turned
        m1[rows, :] = new_first
        m2[rows, :] = new_second
        parts.append(new_first / (jnp.sqrt(new_second) + ADAM_EPS))
    stores = [
        pltpu.make_async_copy(m1, nm_out, osem.at[0]),
        pltpu.make_async_copy(m2, nv_out, osem.at[1]),
    ]
    for store in stores:
        store.start()
    put_half(work, parts)
    put_whole(work, dot((qlh[...], qll[...]), split(whole(work))))
    for p in range(8):
        for r in range(3):
            rows = pl.ds((3 * p + r) * 8, 8)
            for c in range(2):
                lanes = pl.ds(128 * c, 128)
                wp[0, rows, lanes] = work[c, every(48 * p + r, 8, 6), :]
                wp[1, rows, lanes] = work[c, every(6 * p + 3 + r, 8, 48), :]
    swap_w = remote(wp.at[1 - h], wr, ws, wrv, partner)
    swap_w.start()

    @pl.when(first)
    def _():
        zhigh[...], zlow[...] = grad_parts

    @pl.when(jnp.logical_not(first))
    def _():
        zhigh[...], zlow[...] = grad_parts[0].T, grad_parts[1].T

    z = zhigh[...], zlow[...]
    stat = 0.5 * whole(sfull) + 0.5 * symmetric(z, NT)

    swap_w.wait()
    mine = dot(split(wp[h]), split(whole(rhalf.at[h])), NT)
    us[...] = (mine + dot(split(wr[...]), split(whole(rhalf.at[1 - h])), NT)).reshape(8, 3, 8, B)

    def back_one(i):
        p = (a + i) & 7
        return remote(us.at[p], back.at[a], r1s.at[p], r1r.at[a], along_one(p))

    def start_back(i, carry):
        back_one(nth(8 - i)).start()
        return carry

    lax.fori_loop(1, 8, start_back, 0)
    keep = pltpu.make_async_copy(us.at[a], back.at[a], own)
    keep.start()

    put_whole(sfull, stat)
    power = dot(split(stat), (qoh[...], qol[...]))
    scale = 1.0 / jnp.sqrt(jnp.sum(power * power) + NORM_EPS)
    x = power * scale
    flat_full(sfull, nflat.at[0], nflat.at[1])

    def halves_out(flat, left_out, right_out, sem, send, recv):
        @pl.when(first)
        def _():
            pltpu.make_async_copy(flat.at[0], left_out, sem).start()
            remote(flat.at[1], left_out, send, recv, partner).start()

        @pl.when(jnp.logical_not(first))
        def _():
            pltpu.make_async_copy(flat.at[1], right_out, sem).start()
            remote(flat.at[0], right_out, send, recv, partner).start()

    def halves_wait(flat, left_out, right_out, sem, send, recv):
        pltpu.make_async_copy(flat.at[0], left_out, sem).wait()

        @pl.when(first)
        def _():
            remote(flat.at[1], right_out, send, recv, partner).wait()

        @pl.when(jnp.logical_not(first))
        def _():
            remote(flat.at[0], left_out, send, recv, partner).wait()

    halves_out(nflat, nl_out, nr_out, osem.at[2], ts.at[0], tr.at[0])

    def quintic(x):
        parts = split(x)
        gram = symmetric(parts, NT)
        poly = CUBIC_COEFF * gram + QUINTIC_COEFF * symmetric(split(gram), NN)
        return LINEAR_COEFF * x + dot(split(poly), parts)

    x = quintic(quintic(quintic(x)))

    def landed(i, carry):
        s = (a + i) & 7
        remote(us.at[s], back.at[s], r1s.at[s], r1r.at[s], along_one(s)).wait()
        return carry

    lax.fori_loop(1, 8, landed, 0)
    keep.wait()
    for s in range(8):
        for r in range(3):
            for c in range(3):
                pack[c, every(r * 8 + s, 8, 24), :] = back[s, r, :, 128 * c : 128 * c + 128]

    def back_two(i):
        q = (b + i) & 7
        return remote(pack.at[:, pl.ds(pl.multiple_of(q * 24, 8), 24), :], ub.at[b], r2s.at[q], r2r.at[b], along_two(q))

    def start_two(i, carry):
        back_two(nth(8 - i)).start()
        return carry

    lax.fori_loop(1, 8, start_two, 0)
    keep_two = pltpu.make_async_copy(pack.at[:, pl.ds(pl.multiple_of(b * 24, 8), 24), :], ub.at[b], own)
    keep_two.start()

    x = quintic(quintic(x))
    put_whole(xbuf, x)
    flat_full(xbuf, xflat.at[0], xflat.at[1])
    halves_out(xflat, ql_out, qr_out, osem.at[3], ts.at[1], tr.at[1])

    def sent(i, carry):
        p = (a + i) & 7
        q = (b + i) & 7
        remote(gs.at[p], hop.at[a], p1s.at[p], p1r.at[a], along_one(p)).wait_send()
        remote(gbuf.at[h, q], gbuf.at[h, q], p2s.at[q], p2r.at[q], along_two(q)).wait_send()
        return carry

    lax.fori_loop(1, 8, sent, 0)

    def sent_cross(k, carry):
        cross(k).wait_send()
        return carry

    lax.fori_loop(0, 8, sent_cross, 0)
    for store in stores:
        store.wait()
    halves_wait(nflat, nl_out, nr_out, osem.at[2], ts.at[0], tr.at[0])


    def arrived(i, carry):
        q = (b + i) & 7
        remote(
            pack.at[:, pl.ds(pl.multiple_of(q * 24, 8), 24), :], ub.at[q], r2s.at[q], r2r.at[q], along_two(q)
        ).wait()
        return carry

    lax.fori_loop(1, 8, arrived, 0)
    keep_two.wait()

    @pl.when(first)
    def _():
        for k in range(8):
            for r in range(3):
                for c in range(3):
                    upd[c, every(64 * r + k, 8, 8), :] = ub[k, c, pl.ds(8 * r, 8), :]

    @pl.when(jnp.logical_not(first))
    def _():
        for k in range(8):
            for r in range(3):
                for c in range(3):
                    upd[c, pl.ds(64 * r + 8 * k, 8), :] = ub[k, c, pl.ds(8 * r, 8), :]

    lasts = [
        pltpu.make_async_copy(upd.at[c], upd_out.at[:, pl.ds(128 * c, 128)], osem.at[4 + c]) for c in range(3)
    ]
    for last in lasts:
        last.start()

    halves_wait(xflat, ql_out, qr_out, osem.at[3], ts.at[1], tr.at[1])
    for last in lasts:
        last.wait()


def hand_out(*refs):
    copies = [pltpu.make_async_copy(refs[i], refs[7 + i], refs[14].at[i]) for i in range(7)]
    for copy in copies:
        copy.start()
    for copy in copies:
        copy.wait()


def step(grads, *flats):
    tiles = (LINES, 128)
    square = (B, B)
    dma = pltpu.SemaphoreType.DMA
    scratch = [
        pltpu.VMEM((8, 3, 8, B), F32),
        pltpu.VMEM((8, 3, 8, B), F32),
        pltpu.VMEM((2, 8, 3, 8, B), F32),
        pltpu.VMEM((3, B, 128), F32),
        pltpu.VMEM((2, *tiles), F32),
        pltpu.VMEM((2, *tiles), F32),
        pltpu.VMEM((2, *tiles), F32),
        pltpu.VMEM(tiles, F32),
        pltpu.VMEM(tiles, F32),
        pltpu.VMEM((3, B, 128), F32),
        pltpu.VMEM((2, 3, B, 128), F32),
        pltpu.VMEM((2, 2, B, 128), F32),
        pltpu.VMEM((2, B, 128), F32),
        *[pltpu.VMEM(square, BF16)] * 2,
        pltpu.VMEM((3, B, 128), F32),
        pltpu.VMEM((2, 192, 256), F32),
        pltpu.VMEM((192, 256), F32),
        pltpu.VMEM((8, 3, 8, B), F32),
        pltpu.VMEM((8, 3, 8, B), F32),
        pltpu.VMEM((3, 192, 128), F32),
        pltpu.VMEM((8, 3, 24, 128), F32),
        pltpu.VMEM((3, 192, 128), F32),
        pltpu.VMEM((2, *tiles), F32),
        pltpu.VMEM((2, *tiles), F32),
        *[pltpu.VMEM(square, BF16)] * 6,
        dma((5,)),
        dma,
        dma((3,)),
        dma((3,)),
        *[dma((8,))] * 4,
        dma,
        *[dma((8,))] * 2,
        *[dma] * 2,
        *[dma((8,))] * 4,
        *[dma((2,))] * 2,
        dma((7,)),
    ]
    inside = pl.BlockSpec(memory_space=pltpu.VMEM)
    outside = pl.BlockSpec(memory_space=pltpu.HBM)
    shapes = (jax.ShapeDtypeStruct((192, B), F32), *[jax.ShapeDtypeStruct(tiles, F32)] * 6)
    held = pl.pallas_call(
        kernel,
        out_shape=shapes,
        in_specs=[outside] * 7,
        out_specs=(inside,) * 7,
        scratch_shapes=scratch,
        compiler_params=pltpu.CompilerParams(collective_id=0, has_side_effects=True, vmem_limit_bytes=VMEM_BYTES),
        name="soap_step",
    )(*[pltpu.with_memory_space_constraint(x, pltpu.HBM) for x in (grads.transpose(1, 0, 2).reshape(3, 8, 8, B), *[x.reshape(tiles) for x in flats])])
    outs = pl.pallas_call(
        hand_out,
        out_shape=shapes,
        in_specs=[inside] * 7,
        out_specs=(outside,) * 7,
        scratch_shapes=[dma((7,))],
        compiler_params=pltpu.CompilerParams(vmem_limit_bytes=VMEM_BYTES),
        name="hand_out",
    )(*held)
    return (outs[0].reshape(3, 64, B).transpose(1, 0, 2), *[x.reshape(1, -1) for x in outs[1:]])


def solution(mesh):
    specs = (P("tensor", "shard", None), *[P(("tensor", "shard"), None)] * 6)
    return jax.shard_map(step, mesh=mesh, in_specs=specs, out_specs=specs, check_vma=False)
```

```python
import jax
import jax.numpy as jnp
from jax import lax
from jax.experimental import pallas as pl
from jax.experimental.pallas import tpu as pltpu
from jax.sharding import PartitionSpec as P

NS_ITERS = 5
BETA_ONE = 0.9
BETA_TWO = 0.95
ADAM_EPS = 1e-08
NORM_EPS = 1e-06
LINEAR_COEFF = 3.4445
CUBIC_COEFF = -4.775
QUINTIC_COEFF = 2.0315

B = 384
LINES = 576
VMEM_BYTES = 30 << 20
MESH = pl.DeviceIdType.MESH
F32 = jnp.float32
BF16 = jnp.bfloat16
NN = (((1,), (0,)), ((), ()))
NT = (((1,), (1,)), ((), ()))


def split(x):
    high = x.astype(BF16)
    return high, (x - high.astype(F32)).astype(BF16)


def dot(a, b, dims=NN):
    wide = b[0].shape[1 - dims[0][1][0]]
    if wide == B and a[0].shape[0] == B:
        both = lax.dot_general(a[0], jnp.concatenate([b[0], b[1]], 1 - dims[0][1][0]), dims, preferred_element_type=F32)
        cross = lax.dot_general(a[1], b[0], dims, preferred_element_type=F32)
        return both[:, :wide] + (both[:, wide:] + cross)
    left = jnp.concatenate([a[0], a[0], a[1]], dims[0][0][0])
    right = jnp.concatenate([b[0], b[1], b[0]], dims[0][1][0])
    return lax.dot_general(left, right, dims, preferred_element_type=F32)


def symmetric(a, dims):
    cut = 256
    inner = tuple(x[:cut] if dims is NT else x[:, :cut] for x in a)
    corner = dot(tuple(x[:cut] for x in a), inner, dims)
    rows = dot(tuple(x[cut:] for x in a), a, dims)
    return jnp.concatenate([jnp.concatenate([corner, rows[:, :cut].T], 1), rows], 0)


def every(start, count, stride):
    return pl.ds(start, count, stride=stride)


def swap_halves(x):
    return pltpu.roll(x, 64, 1)


def lower():
    return lax.broadcasted_iota(jnp.int32, (192, 128), 1) < 64


def thirds(ref):
    return ref[every(0, 192, 3), :], ref[every(1, 192, 3), :], ref[every(2, 192, 3), :]


def put_thirds(ref, parts):
    for i in range(3):
        ref[every(i, 192, 3), :] = parts[i]


def whole(ref):
    return jnp.concatenate([ref[i] for i in range(ref.shape[0])], 1)


def put_whole(ref, x):
    for i in range(ref.shape[0]):
        ref[i] = x[:, 128 * i : 128 * i + 128]


def put_half(dst, parts):
    a, b, c = parts
    low = lower()
    zero = jnp.zeros((192, 128), F32)
    even, odd = every(0, 192, 2), every(1, 192, 2)
    cs = swap_halves(c)
    dst[0, even, :] = a
    dst[1, even, :] = jnp.where(low, b, zero)
    dst[0, odd, :] = jnp.where(low, swap_halves(b), cs)
    dst[1, odd, :] = jnp.where(low, cs, zero)


def get_half(src):
    low = lower()
    even, odd = every(0, 192, 2), every(1, 192, 2)
    os = swap_halves(src[0, odd, :])
    return (
        src[0, even, :],
        jnp.where(low, src[1, even, :], os),
        jnp.where(low, os, swap_halves(src[1, odd, :])),
    )


def put_full(dst, first, second):
    a0, b0, c0 = thirds(first)
    a1, b1, c1 = thirds(second)
    low = lower()
    even, odd = every(0, 192, 2), every(1, 192, 2)
    a1s, c0s = swap_halves(a1), swap_halves(c0)
    dst[0, even, :] = a0
    dst[1, even, :] = jnp.where(low, b0, a1s)
    dst[2, even, :] = jnp.where(low, a1s, swap_halves(b1))
    dst[0, odd, :] = jnp.where(low, swap_halves(b0), c0s)
    dst[1, odd, :] = jnp.where(low, c0s, b1)
    dst[2, odd, :] = c1


def flat_full(src, first, second):
    low = lower()
    even, odd = every(0, 192, 2), every(1, 192, 2)
    e0, e1, e2 = (src[i, even, :] for i in range(3))
    o0, o1, o2 = (src[i, odd, :] for i in range(3))
    o0s, e2s = swap_halves(o0), swap_halves(e2)
    put_thirds(first, (e0, jnp.where(low, e1, o0s), jnp.where(low, o0s, swap_halves(o1))))
    put_thirds(second, (jnp.where(low, swap_halves(e1), e2s), jnp.where(low, e2s, o1), o2))


def nth(i):
    return jnp.where((i & 1) == 1, (i + 1) // 2, 8 - i // 2)


def kernel(
    g_in, m1_in, m2_in, ls_in, rs_in, lb_in, rb_in,
    upd_out, nm_out, nv_out, nl_out, nr_out, ql_out, qr_out,
    gs, hop, gbuf, gfull, sraw, lraw, rraw, m1, m2, sfull, qfull, rhalf, work, zhigh, zlow, xbuf,
    wp, wr, us, back, pack, ub, upd, nflat, xflat,
    qlh, qll, qth, qtl, qoh, qol,
    lsem, gsem, ssend, srecv, p1s, p1r, p2s, p2r, own, xs, xr, ws, wrv, r1s, r1r, r2s, r2r, ts, tr, osem,
):
    me, t = lax.axis_index("shard"), lax.axis_index("tensor")
    h = me & 1
    chip = me // 2
    cy, cz = chip // 8, chip & 7
    first = h == 0
    a = jnp.where(first, cy, cz)
    b = jnp.where(first, cz, cy)

    def along_one(p):
        return 2 * jnp.where(first, p * 8 + cz, cy * 8 + p) + h

    def along_two(q):
        return 2 * jnp.where(first, cy * 8 + q, q * 8 + cz) + h

    partner = me + 1 - 2 * h

    def remote(src, dst, send, recv, device):
        return pltpu.make_async_remote_copy(
            src_ref=src, dst_ref=dst, send_sem=send, recv_sem=recv, device_id=(device, t), device_id_type=MESH
        )

    barrier = pltpu.get_barrier_semaphore()

    def greet(device):
        pl.semaphore_signal(barrier, inc=1, device_id=(device, t), device_id_type=MESH)

    def greetings(i, carry):
        greet(along_one((a + i) & 7))
        greet(along_two((b + i) & 7))
        return carry

    lax.fori_loop(1, 8, greetings, 0)
    greet(partner)

    def stage(p, carry):
        @pl.when(first)
        def _():
            pltpu.make_async_copy(g_in.at[:, p, :, :], gs.at[p], gsem).start()

        @pl.when(jnp.logical_not(first))
        def _():
            pltpu.make_async_copy(g_in.at[:, :, p, :], gs.at[p], gsem).start()

        return carry

    lax.fori_loop(0, 8, stage, 0)

    @pl.when(first)
    def _():
        pltpu.make_async_copy(ls_in, sraw.at[0], lsem.at[0]).start()

    @pl.when(jnp.logical_not(first))
    def _():
        pltpu.make_async_copy(rs_in, sraw.at[1], lsem.at[0]).start()

    loads = [
        pltpu.make_async_copy(ls_in, sraw.at[h], lsem.at[0]),
        pltpu.make_async_copy(lb_in, lraw.at[h], lsem.at[1]),
        pltpu.make_async_copy(rb_in, rraw.at[h], lsem.at[2]),
        pltpu.make_async_copy(m1_in, m1, lsem.at[3]),
        pltpu.make_async_copy(m2_in, m2, lsem.at[4]),
    ]
    for load in loads[1:]:
        load.start()
    pltpu.make_async_copy(gs, gs, gsem).wait()
    pl.semaphore_wait(barrier, 15)

    def hop_one(i):
        p = (a + i) & 7
        return remote(gs.at[p], hop.at[a], p1s.at[p], p1r.at[a], along_one(p))

    def start_one(i, carry):
        hop_one(nth(8 - i)).start()
        return carry

    lax.fori_loop(1, 8, start_one, 0)

    def forward(src, s):
        def send(i, carry):
            q = (b + nth(8 - i)) & 7
            remote(
                src.at[:, pl.ds(q, 1), :], gbuf.at[h, b, :, pl.ds(s, 1), :], p2s.at[q], p2r.at[b], along_two(q)
            ).start()
            return carry

        lax.fori_loop(1, 8, send, 0)
        pltpu.make_async_copy(src.at[:, pl.ds(b, 1), :], gbuf.at[h, b, :, pl.ds(s, 1), :], own).start()

    forward(gs.at[a], a)

    swaps = [
        remote(lb_in, lraw.at[h], ssend.at[1], srecv.at[1], partner),
        remote(rb_in, rraw.at[h], ssend.at[2], srecv.at[2], partner),
    ]
    for copy in swaps:
        copy.start()

    @pl.when(first)
    def _():
        remote(rs_in, sraw.at[h], ssend.at[0], srecv.at[0], partner).start()

    @pl.when(jnp.logical_not(first))
    def _():
        remote(ls_in, sraw.at[h], ssend.at[0], srecv.at[0], partner).start()

    swap_stat = remote(ls_in, sraw.at[h], ssend.at[0], srecv.at[0], partner)

    def relay(i, carry):
        s = (a + nth(i)) & 7
        remote(gs.at[s], hop.at[s], p1s.at[s], p1r.at[s], along_one(s)).wait_recv()
        forward(hop.at[s], s)
        return carry

    lax.fori_loop(1, 8, relay, 0)

    for load in loads:
        load.wait()
    for copy in swaps:
        copy.wait()
    swap_stat.wait()
    put_full(qfull.at[0], lraw.at[0], lraw.at[1])
    put_full(qfull.at[1], rraw.at[0], rraw.at[1])
    put_full(sfull, sraw.at[0], sraw.at[1])
    put_half(rhalf.at[0], thirds(rraw.at[0]))
    put_half(rhalf.at[1], thirds(rraw.at[1]))
    left = whole(qfull.at[0])
    qlh[...], qll[...] = split(left)
    qth[...], qtl[...] = split(left.T)
    qoh[...], qol[...] = split(whole(qfull.at[h]))

    pltpu.make_async_copy(gbuf.at[0, 0], gbuf.at[0, 0], own).wait()

    def cross(k):
        return remote(gbuf.at[h, k], gbuf.at[h, k], xs.at[k], xr.at[k], partner)

    cross(b).start()

    def pass_on(i, carry):
        k = (b + nth(i)) & 7
        remote(gbuf.at[h, k], gbuf.at[h, k], p2s.at[k], p2r.at[k], along_two(k)).wait_recv()
        cross(k).start()
        return carry

    lax.fori_loop(1, 8, pass_on, 0)

    def crossed(k, carry):
        remote(gbuf.at[1 - h, k], gbuf.at[1 - h, k], xs.at[k], xr.at[k], partner).wait_recv()
        return carry

    lax.fori_loop(0, 8, crossed, 0)
    for k in range(8):
        for r in range(3):
            for c in range(3):
                lanes = pl.ds(128 * c, 128)
                gfull[c, every(6 * k + r, 8, 48), :] = gbuf[0, k, r, :, lanes]
                gfull[c, every(48 * k + 3 + r, 8, 6), :] = gbuf[1, k, r, :, lanes]
    grad_parts = split(whole(gfull))

    rot = dot((qth[...], qtl[...]), split(dot(grad_parts, split(whole(rhalf.at[h])))))
    put_whole(work, rot)
    parts = []
    for i, turned in enumerate(get_half(work)):
        rows = every(i, 192, 3)
        new_first = BETA_ONE * m1[rows, :] + (1.0 - BETA_ONE) * turned
        new_second = BETA_TWO * m2[rows, :] + (1.0 - BETA_TWO) * turned * turned
        m1[rows, :] = new_first
        m2[rows, :] = new_second
        parts.append(new_first / (jnp.sqrt(new_second) + ADAM_EPS))
    stores = [
        pltpu.make_async_copy(m1, nm_out, osem.at[0]),
        pltpu.make_async_copy(m2, nv_out, osem.at[1]),
    ]
    for store in stores:
        store.start()
    put_half(work, parts)
    put_whole(work, dot((qlh[...], qll[...]), split(whole(work))))
    for p in range(8):
        for r in range(3):
            rows = pl.ds((3 * p + r) * 8, 8)
            for c in range(2):
                lanes = pl.ds(128 * c, 128)
                wp[0, rows, lanes] = work[c, every(48 * p + r, 8, 6), :]
                wp[1, rows, lanes] = work[c, every(6 * p + 3 + r, 8, 48), :]
    swap_w = remote(wp.at[1 - h], wr, ws, wrv, partner)
    swap_w.start()

    @pl.when(first)
    def _():
        zhigh[...], zlow[...] = grad_parts

    @pl.when(jnp.logical_not(first))
    def _():
        zhigh[...], zlow[...] = grad_parts[0].T, grad_parts[1].T

    z = zhigh[...], zlow[...]
    stat = 0.5 * whole(sfull) + 0.5 * symmetric(z, NT)

    swap_w.wait()
    mine = dot(split(wp[h]), split(whole(rhalf.at[h])), NT)
    us[...] = (mine + dot(split(wr[...]), split(whole(rhalf.at[1 - h])), NT)).reshape(8, 3, 8, B)

    def back_one(i):
        p = (a + i) & 7
        return remote(us.at[p], back.at[a], r1s.at[p], r1r.at[a], along_one(p))

    def start_back(i, carry):
        back_one(nth(8 - i)).start()
        return carry

    lax.fori_loop(1, 8, start_back, 0)
    keep = pltpu.make_async_copy(us.at[a], back.at[a], own)
    keep.start()

    put_whole(sfull, stat)
    power = dot(split(stat), (qoh[...], qol[...]))
    scale = 1.0 / jnp.sqrt(jnp.sum(power * power) + NORM_EPS)
    x = power * scale
    flat_full(sfull, nflat.at[0], nflat.at[1])

    def halves_out(flat, left_out, right_out, sem, send, recv):
        @pl.when(first)
        def _():
            pltpu.make_async_copy(flat.at[0], left_out, sem).start()
            remote(flat.at[1], left_out, send, recv, partner).start()

        @pl.when(jnp.logical_not(first))
        def _():
            pltpu.make_async_copy(flat.at[1], right_out, sem).start()
            remote(flat.at[0], right_out, send, recv, partner).start()

    def halves_wait(flat, left_out, right_out, sem, send, recv):
        pltpu.make_async_copy(flat.at[0], left_out, sem).wait()

        @pl.when(first)
        def _():
            remote(flat.at[1], right_out, send, recv, partner).wait()

        @pl.when(jnp.logical_not(first))
        def _():
            remote(flat.at[0], left_out, send, recv, partner).wait()

    halves_out(nflat, nl_out, nr_out, osem.at[2], ts.at[0], tr.at[0])

    def quintic(x):
        parts = split(x)
        gram = symmetric(parts, NT)
        poly = CUBIC_COEFF * gram + QUINTIC_COEFF * symmetric(split(gram), NN)
        return LINEAR_COEFF * x + dot(split(poly), parts)

    x = quintic(quintic(quintic(x)))

    def landed(i, carry):
        s = (a + i) & 7
        remote(us.at[s], back.at[s], r1s.at[s], r1r.at[s], along_one(s)).wait()
        return carry

    lax.fori_loop(1, 8, landed, 0)
    keep.wait()
    for s in range(8):
        for r in range(3):
            for c in range(3):
                pack[c, every(r * 8 + s, 8, 24), :] = back[s, r, :, 128 * c : 128 * c + 128]

    def back_two(i):
        q = (b + i) & 7
        return remote(pack.at[:, pl.ds(pl.multiple_of(q * 24, 8), 24), :], ub.at[b], r2s.at[q], r2r.at[b], along_two(q))

    def start_two(i, carry):
        back_two(nth(8 - i)).start()
        return carry

    lax.fori_loop(1, 8, start_two, 0)
    keep_two = pltpu.make_async_copy(pack.at[:, pl.ds(pl.multiple_of(b * 24, 8), 24), :], ub.at[b], own)
    keep_two.start()

    x = quintic(quintic(x))
    put_whole(xbuf, x)
    flat_full(xbuf, xflat.at[0], xflat.at[1])
    halves_out(xflat, ql_out, qr_out, osem.at[3], ts.at[1], tr.at[1])

    def sent(i, carry):
        p = (a + i) & 7
        q = (b + i) & 7
        remote(gs.at[p], hop.at[a], p1s.at[p], p1r.at[a], along_one(p)).wait_send()
        remote(gbuf.at[h, q], gbuf.at[h, q], p2s.at[q], p2r.at[q], along_two(q)).wait_send()
        return carry

    lax.fori_loop(1, 8, sent, 0)

    def sent_cross(k, carry):
        cross(k).wait_send()
        return carry

    lax.fori_loop(0, 8, sent_cross, 0)
    for store in stores:
        store.wait()
    halves_wait(nflat, nl_out, nr_out, osem.at[2], ts.at[0], tr.at[0])


    def arrived(i, carry):
        q = (b + i) & 7
        remote(
            pack.at[:, pl.ds(pl.multiple_of(q * 24, 8), 24), :], ub.at[q], r2s.at[q], r2r.at[q], along_two(q)
        ).wait()
        return carry

    lax.fori_loop(1, 8, arrived, 0)
    keep_two.wait()

    @pl.when(first)
    def _():
        for k in range(8):
            for r in range(3):
                for c in range(3):
                    upd[c, every(64 * r + k, 8, 8), :] = ub[k, c, pl.ds(8 * r, 8), :]

    @pl.when(jnp.logical_not(first))
    def _():
        for k in range(8):
            for r in range(3):
                for c in range(3):
                    upd[c, pl.ds(64 * r + 8 * k, 8), :] = ub[k, c, pl.ds(8 * r, 8), :]

    lasts = [
        pltpu.make_async_copy(upd.at[c], upd_out.at[:, pl.ds(128 * c, 128)], osem.at[4 + c]) for c in range(3)
    ]
    for last in lasts:
        last.start()

    halves_wait(xflat, ql_out, qr_out, osem.at[3], ts.at[1], tr.at[1])
    for last in lasts:
        last.wait()


def hand_out(*refs):
    copies = [pltpu.make_async_copy(refs[i], refs[7 + i], refs[14].at[i]) for i in range(7)]
    for copy in copies:
        copy.start()
    for copy in copies:
        copy.wait()


def step(grads, *flats):
    tiles = (LINES, 128)
    square = (B, B)
    dma = pltpu.SemaphoreType.DMA
    scratch = [
        pltpu.VMEM((8, 3, 8, B), F32),
        pltpu.VMEM((8, 3, 8, B), F32),
        pltpu.VMEM((2, 8, 3, 8, B), F32),
        pltpu.VMEM((3, B, 128), F32),
        pltpu.VMEM((2, *tiles), F32),
        pltpu.VMEM((2, *tiles), F32),
        pltpu.VMEM((2, *tiles), F32),
        pltpu.VMEM(tiles, F32),
        pltpu.VMEM(tiles, F32),
        pltpu.VMEM((3, B, 128), F32),
        pltpu.VMEM((2, 3, B, 128), F32),
        pltpu.VMEM((2, 2, B, 128), F32),
        pltpu.VMEM((2, B, 128), F32),
        *[pltpu.VMEM(square, BF16)] * 2,
        pltpu.VMEM((3, B, 128), F32),
        pltpu.VMEM((2, 192, 256), F32),
        pltpu.VMEM((192, 256), F32),
        pltpu.VMEM((8, 3, 8, B), F32),
        pltpu.VMEM((8, 3, 8, B), F32),
        pltpu.VMEM((3, 192, 128), F32),
        pltpu.VMEM((8, 3, 24, 128), F32),
        pltpu.VMEM((3, 192, 128), F32),
        pltpu.VMEM((2, *tiles), F32),
        pltpu.VMEM((2, *tiles), F32),
        *[pltpu.VMEM(square, BF16)] * 6,
        dma((5,)),
        dma,
        dma((3,)),
        dma((3,)),
        *[dma((8,))] * 4,
        dma,
        *[dma((8,))] * 2,
        *[dma] * 2,
        *[dma((8,))] * 4,
        *[dma((2,))] * 2,
        dma((7,)),
    ]
    inside = pl.BlockSpec(memory_space=pltpu.VMEM)
    outside = pl.BlockSpec(memory_space=pltpu.HBM)
    shapes = (jax.ShapeDtypeStruct((192, B), F32), *[jax.ShapeDtypeStruct(tiles, F32)] * 6)
    held = pl.pallas_call(
        kernel,
        out_shape=shapes,
        in_specs=[outside] * 7,
        out_specs=(inside,) * 7,
        scratch_shapes=scratch,
        compiler_params=pltpu.CompilerParams(
            collective_id=0,
            has_side_effects=True,
            vmem_limit_bytes=VMEM_BYTES,
        ),
        name="soap_step",
    )(*[pltpu.with_memory_space_constraint(x, pltpu.HBM) for x in (grads.transpose(1, 0, 2).reshape(3, 8, 8, B), *[x.reshape(tiles) for x in flats])])
    outs = pl.pallas_call(
        hand_out,
        out_shape=shapes,
        in_specs=[inside] * 7,
        out_specs=(outside,) * 7,
        scratch_shapes=[dma((7,))],
        compiler_params=pltpu.CompilerParams(vmem_limit_bytes=VMEM_BYTES),
        name="hand_out",
    )(*held)
    return (outs[0].reshape(3, 64, B).transpose(1, 0, 2), *[x.reshape(1, -1) for x in outs[1:]])


def solution(mesh):
    specs = (P("tensor", "shard", None), *[P(("tensor", "shard"), None)] * 6)
    return jax.shard_map(step, mesh=mesh, in_specs=specs, out_specs=specs, check_vma=False)
```
